32 devices in a mesh: tiles: 2 (over x), disp: 8 (over z, y), rows: 2 (over core).
Axes of the slice: x: 2, y: 2, z: 4, core: 2. Of those that a mesh axis runs over, the one named last changes fastest.
Arguments:
- volume: bfloat16 [32, 192, 64, 512], P(None, 'disp', ('tiles', 'rows')), parts along dimension 2, may hold values from -1000 to 1000, as said below
- conv_weight: bfloat16 [27, 32, 32], replicated, may hold values from -0.21875 to 0.21875
- conv_bias: float32 [32], replicated, may hold values from -3 to 3
- reg_weight: bfloat16 [27, 32], replicated, may hold values from -0.875 to 0.875
Outputs:
- disparity: float32 [64, 512], P(('tiles', 'rows')), parts along dimension 0
The draws below stay inside these ranges and needn't reach their ends.
There are 2 independent parts, one for each index of `tiles`. The reference program is written for one: setup_inputs(seed, part) draws one part's arguments, and reference() takes and returns one part's arrays. A program takes and returns all parts, laid end to end along the dimension named above; an argument that names none is the same for every part. Nothing has to cross between parts.
Inputs may be any that keep to these rules, and one draw needn't show every extreme that they name: `volume`: Real-valued matching features.
All inputs are finite; a program needn't handle non-finite values.
Results may differ from the reference program's by a relative error of at most 0.008.
Values may be sent and summed in bfloat16 or wider, within the bound.
A program may use at most 384 MiB of HBM per device.

```python
import jax
import jax.numpy as jnp
from jax import lax

CH = 32
DISP = 192
WIDTH = 512
ROWS = 32


def draw_volume(key, part):
    first = jax.random.fold_in(jax.random.fold_in(key, 7), 0)
    base = jnp.clip(jax.random.normal(first, (CH, DISP, ROWS, WIDTH), jnp.float32), -6.0, 6.0)
    return base.astype(jnp.bfloat16)


def bell_draw(key, dims, deviation, limit, held_as=jnp.bfloat16):
    drawn = deviation * jax.random.normal(key, dims, jnp.float32)
    return jnp.clip(drawn, min=-limit, max=limit).astype(held_as)


def setup_inputs(seed: int = 0, part: int = 0) -> dict:
    splits = jax.random.split(jax.random.key(seed), 5)
    part_splits = jax.random.split(jax.random.fold_in(splits[4], part), 5)
    volume = draw_volume(jax.random.fold_in(jax.random.fold_in(splits[4], part), 71), part)
    conv_weight = bell_draw(splits[1], (27, CH, CH), (27 * CH) ** -0.5, 0.21875)
    conv_bias = bell_draw(splits[2], (CH,), 0.5, 3.0, jnp.float32)
    reg_weight = bell_draw(splits[3], (27, CH), (27 * CH // 16) ** -0.5, 0.875)
    return {"volume": volume, "conv_weight": conv_weight, "conv_bias": conv_bias, "reg_weight": reg_weight}


def aggregate(volume, conv_weight, conv_bias):
    padded = jnp.pad(volume, ((0, 0), (1, 1), (1, 1), (1, 1))).astype(jnp.float32)
    weights = conv_weight.astype(jnp.float32)
    summed = jnp.zeros((CH, DISP, ROWS, WIDTH), jnp.float32)
    for depth_tap in range(3):
        for row_tap in range(3):
            for col_tap in range(3):
                window = padded[:, depth_tap:depth_tap + DISP, row_tap:row_tap + ROWS, col_tap:col_tap + WIDTH]
                summed = summed + jnp.einsum("oc,cdhw->odhw", weights[9 * depth_tap + 3 * row_tap + col_tap], window, precision=lax.Precision.HIGHEST)
    return jnp.maximum(summed + conv_bias[:, None, None, None], 0.0).astype(jnp.bfloat16)


def regress(hidden, reg_weight):
    padded = jnp.pad(hidden, ((0, 0), (1, 1), (1, 1), (1, 1))).astype(jnp.float32)
    weights = reg_weight.astype(jnp.float32)
    cost = jnp.zeros((DISP, ROWS, WIDTH), jnp.float32)
    for depth_tap in range(3):
        for row_tap in range(3):
            for col_tap in range(3):
                window = padded[:, depth_tap:depth_tap + DISP, row_tap:row_tap + ROWS, col_tap:col_tap + WIDTH]
                cost = cost + jnp.einsum("c,cdhw->dhw", weights[9 * depth_tap + 3 * row_tap + col_tap], window, precision=lax.Precision.HIGHEST)
    return cost


def reference(volume, conv_weight, conv_bias, reg_weight):
    hidden = aggregate(volume, conv_weight, conv_bias)
    cost = regress(hidden, reg_weight)
    score = -cost
    peak = jnp.max(score, axis=0)
    expo = jnp.exp(score - peak[None])
    planes = jnp.arange(DISP).astype(jnp.float32)
    total = jnp.sum(expo, axis=0)
    moment = jnp.sum(planes[:, None, None] * expo, axis=0)
    return moment / total
```

```python
import functools

import jax
import jax.numpy as jnp
from jax import lax
from jax.experimental import pallas as pl
from jax.experimental.pallas import tpu as pltpu
from jax.sharding import PartitionSpec as P

BF = jnp.bfloat16
F32 = jnp.float32


def shifted(x, axis, step):
    count = lax.axis_size(axis)
    pairs = [(i, i + step) for i in range(count) if 0 <= i + step < count]
    return lax.ppermute(x, axis, pairs)


def band_matrix(conv_weight, height):
    ch_out, ch = conv_weight.shape[1:]
    span = ch * height
    col = jnp.arange(span)
    spread = (col[None, :] // height == jnp.arange(ch)[:, None]).astype(BF)
    wide = jnp.einsum("toc,cg->tog", conv_weight, spread, preferred_element_type=F32).astype(BF)
    row = jnp.arange(height)
    masks = [(col[None, :] % height) == row[:, None] + b - 1 for b in range(3)]
    slots = []
    for a in range(3):
        parts = []
        for c in range(3):
            out = jnp.zeros((ch_out, height, span), BF)
            for b in range(3):
                out = jnp.where(masks[b][None], wide[9 * a + 3 * b + c][:, None, :], out)
            parts.append(out.reshape(ch_out * height, span))
        zero = jnp.zeros((ch_out, ch), BF)
        edges = []
        for c in range(3):
            edges += [conv_weight[9 * a + c], conv_weight[9 * a + 6 + c]]
        pad = edge_rows(ch) - 6 * ch
        edges += [jnp.zeros((ch_out, pad), BF)]
        edge = jnp.concatenate(edges, axis=1)
        ecol = jnp.arange(edge_rows(ch))
        side = (ecol // ch) % 2
        keep = row[:, None] == jnp.where(side == 0, 0, height - 1)[None, :]
        edge = jnp.where(keep[None], edge[:, None, :], jnp.zeros((), BF))
        parts.append(edge.reshape(ch_out * height, edge_rows(ch)))
        slots.append(parts)
    return jnp.concatenate([p for a in (0, 1, 2, 0, 1) for p in slots[a]], axis=1)


def edge_rows(ch):
    return -(-6 * ch // 256) * 256


def reg_matrix(reg_weight, height):
    ch = reg_weight.shape[1]
    span = ch * height
    col = jnp.arange(span)
    spread = (col[None, :] // height == jnp.arange(ch)[:, None]).astype(BF)
    wide = jnp.einsum("tc,cg->tg", reg_weight, spread, preferred_element_type=F32).astype(BF)
    row = jnp.arange(height + 8)
    place = jnp.where(row < height, row, jnp.where(row == height, -1, jnp.where(row == height + 1, height, -9)))
    out = []
    for a in range(3):
        for c in range(3):
            block = jnp.zeros((height + 8, span), BF)
            for b in range(3):
                mask = (col[None, :] % height) == place[:, None] + b - 1
                block = jnp.where(mask, wide[9 * a + 3 * b + c][None], block)
            out.append(block)
    return jnp.concatenate(out, axis=0)


def move(x, step):
    width = x.shape[1]
    rolled = pltpu.roll(x, step % width, 1)
    lane = lax.broadcasted_iota(jnp.int32, x.shape, 1)
    return jnp.where(lane == (0 if step == 1 else width - 1), jnp.zeros((), x.dtype), rolled)


def put_plane(x3, slot, x, e):
    span, es = x.shape[0], e.shape[0]
    depth = x3.shape[1]
    for k, step in enumerate((1, 0, -1)):
        if step:
            xs = move(x.astype(F32), step).astype(BF)
            es_ = move(e.astype(F32), step).astype(BF)
        else:
            xs, es_ = x, e
        x3[slot, k * span : (k + 1) * span, :] = xs
        x3[slot, 3 * span + k * es : 3 * span + (k + 1) * es, :] = es_
    tail = 3 * span + 3 * es
    if tail < depth:
        x3[slot, tail:depth, :] = jnp.zeros((depth - tail, x.shape[1]), BF)


def out_plane(phase, a_ref, x3, bias, r_ref, cost, at):
    slots, depth, width = x3.shape
    start = phase * depth if isinstance(phase, int) else pl.multiple_of(phase * depth, 128)
    a = a_ref[:, pl.ds(start, slots * depth)]
    x = x3[...].reshape(slots * depth, width)
    acc = jnp.dot(a, x, preferred_element_type=F32)
    hidden = jnp.maximum(acc + bias[...], 0.0).astype(BF)
    part = jnp.dot(r_ref[...], hidden, preferred_element_type=F32)
    rows = cost.shape[1]
    for tap in range(3):
        base = 3 * tap * rows
        total = (
            move(part[base : base + rows], 1)
            + part[base + rows : base + 2 * rows]
            + move(part[base + 2 * rows : base + 3 * rows], -1)
        )
        cost[at + 2 - tap] += total


def inner_kernel(v_ref, e_ref, a_ref, bias, r_ref, cost, x3):
    step = pl.program_id(0)

    @pl.when(step == 0)
    def _():
        cost[...] = jnp.zeros_like(cost)

    span = v_ref.shape[0] * v_ref.shape[2]
    put_plane(x3, lax.rem(step, 3), v_ref[:, 0].reshape(span, v_ref.shape[3]), e_ref[0])

    @pl.when(step >= 2)
    def _():
        first = lax.rem(step + 1, 3)
        out_plane(lax.rem(3 - first, 3), a_ref, x3, bias, r_ref, cost, step - 1)


def rim_kernel(planes, v_ref, e_ref, a_ref, bias, r_ref, cost_in, cost, x3):
    step = pl.program_id(0)

    @pl.when(step == 0)
    def _():
        cost[...] = cost_in[...]

    span = v_ref.shape[1] * v_ref.shape[2]
    put_plane(x3, lax.rem(step, 3), v_ref[0].reshape(span, v_ref.shape[3]), e_ref[0])

    @pl.when(lax.rem(step, 3) == 2)
    def _():
        out_plane(0, a_ref, x3, bias, r_ref, cost, jnp.where(step == 2, 0, planes - 1))


def combine(first, second):
    peak = jnp.maximum(first[0], second[0])
    left = jnp.exp(first[0] - peak)
    right = jnp.exp(second[0] - peak)
    return jnp.stack((peak, first[1] * left + second[1] * right, first[2] * left + second[2] * right))


def joined(value, axis):
    count = lax.axis_size(axis)
    if count & (count - 1):
        pieces = lax.all_gather(value, axis)
        running = pieces[0]
        for i in range(1, count):
            running = combine(running, pieces[i])
        return running
    step = 1
    while step < count:
        other = lax.ppermute(value, axis, [(i, i ^ step) for i in range(count)])
        value = combine(value, other)
        step *= 2
    return value


def body(volume, conv_weight, conv_bias, reg_weight):
    ch, planes, height, width = volume.shape
    span = ch * height
    rows = height + 8
    depth = 3 * span + edge_rows(ch)

    before = shifted(volume[:, planes - 1], "disp", 1)
    after = shifted(volume[:, 0], "disp", -1)
    above = shifted(jnp.swapaxes(volume[:, :, height - 1], 0, 1), "rows", 1)
    below = shifted(jnp.swapaxes(volume[:, :, 0], 0, 1), "rows", -1)
    edge = jnp.concatenate([above, below], axis=1)
    edge_before = shifted(edge[planes - 1], "disp", 1)
    edge_after = shifted(edge[0], "disp", -1)

    a = band_matrix(conv_weight, height)
    r = reg_matrix(reg_weight, height)
    bias = jnp.repeat(conv_bias, height)[:, None]

    def whole(x):
        return pl.BlockSpec(x.shape, lambda i: (0,) * x.ndim, pipeline_mode=pl.Buffered(1))

    cost_shape = jax.ShapeDtypeStruct((planes + 2, rows, width), F32)
    cost_spec = pl.BlockSpec(cost_shape.shape, lambda i: (0, 0, 0))
    scratch = [pltpu.VMEM((3, depth, width), BF)]
    params = pltpu.CompilerParams(vmem_limit_bytes=56 << 20, dimension_semantics=("arbitrary",))
    flops = 2 * span * 3 * depth * width

    cost = pl.pallas_call(
        inner_kernel,
        grid=(planes,),
        in_specs=[
            pl.BlockSpec((ch, 1, height, width), lambda i: (0, i, 0, 0)),
            pl.BlockSpec((1, 2 * ch, width), lambda i: (i, 0, 0)),
            whole(a),
            whole(bias),
            whole(r),
        ],
        out_specs=cost_spec,
        out_shape=cost_shape,
        scratch_shapes=scratch,
        compiler_params=params,
        cost_estimate=pl.CostEstimate(
            flops=(planes - 2) * flops, bytes_accessed=2 * volume.size, transcendentals=0
        ),
        name="inner",
    )(volume, edge, a, bias, r)

    rim_v = jnp.stack(
        [before, volume[:, 0], volume[:, 1], volume[:, planes - 2], volume[:, planes - 1], after]
    )
    rim_e = jnp.stack([edge_before, edge[0], edge[1], edge[planes - 2], edge[planes - 1], edge_after])
    cost = pl.pallas_call(
        functools.partial(rim_kernel, planes),
        grid=(6,),
        in_specs=[
            pl.BlockSpec((1, ch, height, width), lambda i: (i, 0, 0, 0)),
            pl.BlockSpec((1, 2 * ch, width), lambda i: (i, 0, 0)),
            whole(a),
            whole(bias),
            whole(r),
            whole(cost_shape),
        ],
        out_specs=cost_spec,
        out_shape=cost_shape,
        scratch_shapes=scratch,
        compiler_params=params,
        cost_estimate=pl.CostEstimate(flops=2 * flops, bytes_accessed=2 * rim_v.size, transcendentals=0),
        name="rim",
    )(rim_v, rim_e, a, bias, r, cost)

    from_before = shifted(cost[planes + 1], "disp", 1)
    from_after = shifted(cost[0], "disp", -1)
    cost = cost[1 : planes + 1]
    cost = cost.at[0].add(from_before).at[planes - 1].add(from_after)
    from_below = shifted(cost[:, height], "rows", -1)
    from_above = shifted(cost[:, height + 1], "rows", 1)
    cost = cost[:, :height]
    cost = cost.at[:, height - 1].add(from_below).at[:, 0].add(from_above)

    score = -cost
    peak = jnp.max(score, axis=0)
    expo = jnp.exp(score - peak[None])
    index = (lax.axis_index("disp") * planes + jnp.arange(planes, dtype=jnp.int32)).astype(F32)
    total = jnp.sum(expo, axis=0)
    moment = jnp.sum(index[:, None, None] * expo, axis=0)
    value = joined(jnp.stack((peak, total, moment)), "disp")
    return value[2] / value[1]


def solution(mesh):
    in_specs = (P(None, "disp", ("tiles", "rows"), None), P(), P(), P())
    out_specs = P(("tiles", "rows"), None)
    return jax.shard_map(body, mesh=mesh, in_specs=in_specs, out_specs=out_specs, check_vma=False)
```

```python
import functools

import jax
import jax.numpy as jnp
from jax import lax
from jax.experimental import pallas as pl
from jax.experimental.pallas import tpu as pltpu
from jax.sharding import PartitionSpec as P

BF = jnp.bfloat16
F32 = jnp.float32


def shifted(x, axis, step):
    count = lax.axis_size(axis)
    pairs = [(i, i + step) for i in range(count) if 0 <= i + step < count]
    return lax.ppermute(x, axis, pairs)


def edge_rows(ch):
    return -(-6 * ch // 256) * 256


def spread(rows, half):
    ch = rows.shape[-1]
    col = jnp.arange(ch * half)
    onehot = (col[None, :] // half == jnp.arange(ch)[:, None]).astype(BF)
    return jnp.einsum("...c,cg->...g", rows, onehot, preferred_element_type=F32)


def prep_kernel(v_ref, wide, wedge, wreg, last, first, local, a_ref, r_ref, pick):
    ch, count, height, width = v_ref.shape
    half = height // 2
    span = ch * half
    depth = 3 * span + edge_rows(ch)

    @pl.when(pl.program_id(0) == 0)
    def _():
        row = lax.broadcasted_iota(jnp.int32, pick.shape, 0)
        col = lax.broadcasted_iota(jnp.int32, pick.shape, 1)
        kind = row // ch
        at = jnp.where(kind == 0, height - 1, jnp.where(kind == 1, 0, jnp.where(kind == 2, half, half - 1)))
        pick[...] = (col == (row % ch) * height + at).astype(F32).astype(BF)

        shape = (ch, half, span)
        diff = lax.broadcasted_iota(jnp.int32, shape, 2) % half - lax.broadcasted_iota(jnp.int32, shape, 1)
        eshape = (ch, half, edge_rows(ch))
        side = (lax.broadcasted_iota(jnp.int32, eshape, 2) // ch) % 2
        keep = lax.broadcasted_iota(jnp.int32, eshape, 1) == side * (half - 1)
        for a in range(3):
            for c in range(3):
                out = jnp.zeros(shape, F32)
                for b in range(3):
                    line = jnp.broadcast_to(wide[9 * a + 3 * b + c][:, None, :], shape)
                    out = jnp.where(diff == b - 1, line, out)
                block = out.reshape(span, span).astype(BF)
                for slot in (a, a + 3):
                    if slot < 5:
                        a_ref[:, slot * depth + c * span : slot * depth + (c + 1) * span] = block
            line = jnp.broadcast_to(wedge[a][:, None, :], eshape)
            block = jnp.where(keep, line, 0.0).reshape(span, edge_rows(ch)).astype(BF)
            for slot in (a, a + 3):
                if slot < 5:
                    a_ref[:, slot * depth + 3 * span : (slot + 1) * depth] = block

        rshape = (height + 8, 2 * span)
        row = lax.broadcasted_iota(jnp.int32, rshape, 0)
        col = lax.broadcasted_iota(jnp.int32, rshape, 1)
        place = jnp.where(
            row < height, row, jnp.where(row == height, -1, jnp.where(row == height + 1, height, -9))
        )
        diff = (col // span) * half + col % half - place
        blocks = []
        for a in range(3):
            for c in range(3):
                out = jnp.zeros(rshape, F32)
                for b in range(3):
                    t = 9 * a + 3 * b + c
                    out = jnp.where(diff == b - 1, jnp.broadcast_to(wreg[t : t + 1, :], rshape), out)
                blocks.append(out)
        r_ref[...] = jnp.concatenate(blocks, axis=0).astype(BF)

    for p in range(count):
        x = v_ref[:, p].reshape(ch * height, width)
        rows = jnp.dot(pick[...], x, preferred_element_type=F32).astype(BF)
        last[p] = rows[:ch]
        first[p] = rows[ch : 2 * ch]
        local[p] = rows[2 * ch :]


def move(x, step):
    width = x.shape[1]
    rolled = pltpu.roll(x, step % width, 1)
    lane = lax.broadcasted_iota(jnp.int32, x.shape, 1)
    return jnp.where(lane == (0 if step == 1 else width - 1), jnp.zeros((), x.dtype), rolled)


def moved(x, step):
    return move(x.astype(F32), step).astype(BF) if step else x


def put_half(x3, slot, x, top, bottom):
    span, ch = x.shape[0], top.shape[0]
    depth = x3.shape[1]
    for k, step in enumerate((1, 0, -1)):
        x3[slot, k * span : (k + 1) * span, :] = moved(x, step)
        base = 3 * span + 2 * k * ch
        x3[slot, base : base + ch, :] = moved(top, step)
        x3[slot, base + ch : base + 2 * ch, :] = moved(bottom, step)
    tail = 3 * span + 6 * ch
    if tail < depth:
        x3[slot, tail:depth, :] = jnp.zeros((depth - tail, x.shape[1]), BF)


def out_plane(phase, a_ref, halves, bias, r_ref, cost, at):
    slots, depth, width = halves[0].shape
    start = phase * depth if isinstance(phase, int) else pl.multiple_of(phase * depth, 128)
    hidden = []
    for x3 in halves:
        a = a_ref[:, pl.ds(start, slots * depth)]
        acc = jnp.dot(a, x3[...].reshape(slots * depth, width), preferred_element_type=F32)
        hidden.append(jnp.maximum(acc + bias[...], 0.0).astype(BF))
    part = jnp.dot(r_ref[...], jnp.concatenate(hidden, axis=0), preferred_element_type=F32)
    rows = cost.shape[1]
    for tap in range(3):
        base = 3 * tap * rows
        total = (
            move(part[base : base + rows], 1)
            + part[base + rows : base + 2 * rows]
            + move(part[base + 2 * rows : base + 3 * rows], -1)
        )
        cost[at + 2 - tap] += total


def flat(x):
    return x.reshape(x.shape[0] * x.shape[1], x.shape[2])


def inner_kernel(lo, hi, above, local, below, a_ref, bias, r_ref, cost, x_lo, x_hi):
    step = pl.program_id(0)
    ch = above.shape[1]

    @pl.when(step == 0)
    def _():
        cost[...] = jnp.zeros_like(cost)

    slot = lax.rem(step, 3)
    put_half(x_lo, slot, flat(lo[:, 0]), above[0], local[0, :ch])
    put_half(x_hi, slot, flat(hi[:, 0]), local[0, ch:], below[0])

    @pl.when(step >= 2)
    def _():
        first = lax.rem(step + 1, 3)
        out_plane(lax.rem(3 - first, 3), a_ref, (x_lo, x_hi), bias, r_ref, cost, step - 1)


def rim_kernel(planes, lo, hi, b_lo, b_hi, a_lo, a_hi, e_ref, a_ref, bias, r_ref, cost_in, cost, x_lo, x_hi):
    step = pl.program_id(0)
    ch = lo.shape[0]

    @pl.when(step == 0)
    def _():
        cost[...] = cost_in[...]

    slot = lax.rem(step, 3)

    def put(low, high):
        put_half(x_lo, slot, flat(low), e_ref[0, :ch], e_ref[0, ch : 2 * ch])
        put_half(x_hi, slot, flat(high), e_ref[0, 2 * ch : 3 * ch], e_ref[0, 3 * ch :])

    @pl.when(step == 0)
    def _():
        put(b_lo[...], b_hi[...])

    @pl.when(step == 5)
    def _():
        put(a_lo[...], a_hi[...])

    @pl.when((step != 0) & (step != 5))
    def _():
        put(lo[:, 0], hi[:, 0])

    @pl.when(slot == 2)
    def _():
        out_plane(0, a_ref, (x_lo, x_hi), bias, r_ref, cost, jnp.where(step == 2, 0, planes - 1))


def combine(first, second):
    peak = jnp.maximum(first[0], second[0])
    left = jnp.exp(first[0] - peak)
    right = jnp.exp(second[0] - peak)
    return jnp.stack((peak, first[1] * left + second[1] * right, first[2] * left + second[2] * right))


def joined(value, axis):
    count = lax.axis_size(axis)
    if count & (count - 1):
        pieces = lax.all_gather(value, axis)
        running = pieces[0]
        for i in range(1, count):
            running = combine(running, pieces[i])
        return running
    step = 1
    while step < count:
        other = lax.ppermute(value, axis, [(i, i ^ step) for i in range(count)])
        value = combine(value, other)
        step *= 2
    return value


def body(volume, conv_weight, conv_bias, reg_weight):
    ch, planes, height, width = volume.shape
    half = height // 2
    span = ch * half
    rows = height + 8
    depth = 3 * span + edge_rows(ch)

    def whole(x):
        return pl.BlockSpec(x.shape, lambda i: (0,) * len(x.shape), pipeline_mode=pl.Buffered(1))

    def shape(*dims, dtype=BF):
        return jax.ShapeDtypeStruct(dims, dtype)

    before = shifted(volume[:, planes - 1], "disp", 1)
    after = shifted(volume[:, 0], "disp", -1)

    wide = spread(conv_weight, half)
    taps = jnp.transpose(conv_weight.reshape(3, 3, 3, ch, ch)[:, ::2], (0, 3, 2, 1, 4)).reshape(3, ch, 6 * ch)
    wedge = jnp.pad(taps, ((0, 0), (0, 0), (0, edge_rows(ch) - 6 * ch))).astype(F32)
    wreg = jnp.tile(spread(reg_weight, half), (1, 2))
    bias = jnp.repeat(conv_bias, half)[:, None]

    group = next(n for n in (4, 3, 2, 1) if planes % n == 0)
    last, first, local, a, r = pl.pallas_call(
        prep_kernel,
        grid=(planes // group,),
        in_specs=[
            pl.BlockSpec((ch, group, height, width), lambda i: (0, i, 0, 0)),
            whole(wide),
            whole(wedge),
            whole(wreg),
        ],
        out_specs=[
            pl.BlockSpec((group, ch, width), lambda i: (i, 0, 0)),
            pl.BlockSpec((group, ch, width), lambda i: (i, 0, 0)),
            pl.BlockSpec((group, 2 * ch, width), lambda i: (i, 0, 0)),
            pl.BlockSpec((span, 5 * depth), lambda i: (0, 0)),
            pl.BlockSpec((9 * rows, 2 * span), lambda i: (0, 0)),
        ],
        out_shape=[
            shape(planes, ch, width),
            shape(planes, ch, width),
            shape(planes, 2 * ch, width),
            shape(span, 5 * depth),
            shape(9 * rows, 2 * span),
        ],
        scratch_shapes=[pltpu.VMEM((4 * ch, ch * height), BF)],
        compiler_params=pltpu.CompilerParams(vmem_limit_bytes=48 << 20),
        cost_estimate=pl.CostEstimate(
            flops=8 * ch * ch * height * width * planes, bytes_accessed=2 * volume.size, transcendentals=0
        ),
        name="prep",
    )(volume, wide, wedge, wreg)

    above = shifted(last, "rows", 1)
    below = shifted(first, "rows", -1)

    def edges(p):
        return jnp.concatenate([above[p], local[p], below[p]], axis=0)

    head, foot = edges(0), edges(planes - 1)
    edge_before = shifted(foot, "disp", 1)
    edge_after = shifted(head, "disp", -1)

    cost_shape = shape(planes + 2, rows, width, dtype=F32)
    cost_spec = pl.BlockSpec(cost_shape.shape, lambda i: (0, 0, 0))
    scratch = [pltpu.VMEM((3, depth, width), BF)] * 2
    params = pltpu.CompilerParams(vmem_limit_bytes=48 << 20)
    flops = 4 * span * 3 * depth * width

    cost = pl.pallas_call(
        inner_kernel,
        grid=(planes,),
        in_specs=[
            pl.BlockSpec((ch, 1, half, width), lambda i: (0, i, 0, 0)),
            pl.BlockSpec((ch, 1, half, width), lambda i: (0, i, 1, 0)),
            pl.BlockSpec((1, ch, width), lambda i: (i, 0, 0)),
            pl.BlockSpec((1, 2 * ch, width), lambda i: (i, 0, 0)),
            pl.BlockSpec((1, ch, width), lambda i: (i, 0, 0)),
            whole(a),
            whole(bias),
            whole(r),
        ],
        out_specs=cost_spec,
        out_shape=cost_shape,
        scratch_shapes=scratch,
        compiler_params=params,
        cost_estimate=pl.CostEstimate(
            flops=(planes - 2) * flops, bytes_accessed=2 * volume.size, transcendentals=0
        ),
        name="inner",
    )(volume, volume, above, local, below, a, bias, r)

    def rim_plane(i):
        return jnp.where(i < 3, jnp.maximum(i - 1, 0), jnp.minimum(planes + i - 5, planes - 1))

    rim_e = jnp.stack([edge_before, head, edges(1), edges(planes - 2), foot, edge_after])
    cost = pl.pallas_call(
        functools.partial(rim_kernel, planes),
        grid=(6,),
        in_specs=[
            pl.BlockSpec((ch, 1, half, width), lambda i: (0, rim_plane(i), 0, 0)),
            pl.BlockSpec((ch, 1, half, width), lambda i: (0, rim_plane(i), 1, 0)),
            pl.BlockSpec((ch, half, width), lambda i: (0, 0, 0), pipeline_mode=pl.Buffered(1)),
            pl.BlockSpec((ch, half, width), lambda i: (0, 1, 0), pipeline_mode=pl.Buffered(1)),
            pl.BlockSpec((ch, half, width), lambda i: (0, 0, 0), pipeline_mode=pl.Buffered(1)),
            pl.BlockSpec((ch, half, width), lambda i: (0, 1, 0), pipeline_mode=pl.Buffered(1)),
            pl.BlockSpec((1, 4 * ch, width), lambda i: (i, 0, 0)),
            whole(a),
            whole(bias),
            whole(r),
            whole(cost_shape),
        ],
        out_specs=cost_spec,
        out_shape=cost_shape,
        scratch_shapes=scratch,
        compiler_params=params,
        cost_estimate=pl.CostEstimate(flops=2 * flops, bytes_accessed=2 * volume.size // 4, transcendentals=0),
        name="rim",
    )(volume, volume, before, before, after, after, rim_e, a, bias, r, cost)

    from_before = shifted(cost[planes + 1], "disp", 1)
    from_after = shifted(cost[0], "disp", -1)
    cost = cost[1 : planes + 1]
    cost = cost.at[0].add(from_before).at[planes - 1].add(from_after)
    from_below = shifted(cost[:, height], "rows", -1)
    from_above = shifted(cost[:, height + 1], "rows", 1)
    cost = cost[:, :height]
    cost = cost.at[:, height - 1].add(from_below).at[:, 0].add(from_above)

    score = -cost
    peak = jnp.max(score, axis=0)
    expo = jnp.exp(score - peak[None])
    index = (lax.axis_index("disp") * planes + jnp.arange(planes, dtype=jnp.int32)).astype(F32)
    total = jnp.sum(expo, axis=0)
    moment = jnp.sum(index[:, None, None] * expo, axis=0)
    value = joined(jnp.stack((peak, total, moment)), "disp")
    return value[2] / value[1]


def solution(mesh):
    in_specs = (P(None, "disp", ("tiles", "rows"), None), P(), P(), P())
    out_specs = P(("tiles", "rows"), None)
    return jax.shard_map(body, mesh=mesh, in_specs=in_specs, out_specs=out_specs, check_vma=False)
```

```python
import functools

import jax
import jax.numpy as jnp
from jax import lax
from jax.experimental import pallas as pl
from jax.experimental.pallas import tpu as pltpu
from jax.sharding import PartitionSpec as P

BF = jnp.bfloat16
F32 = jnp.float32
MESH = pl.DeviceIdType.MESH


def shifted(x, axis, step):
    count = lax.axis_size(axis)
    pairs = [(i, i + step) for i in range(count) if 0 <= i + step < count]
    return lax.ppermute(x, axis, pairs)


def edge_rows(ch):
    return -(-6 * ch // 256) * 256


def spread(rows, half):
    ch = rows.shape[-1]
    col = jnp.arange(ch * half)
    onehot = (col[None, :] // half == jnp.arange(ch)[:, None]).astype(BF)
    return jnp.einsum("...c,cg->...g", rows, onehot, preferred_element_type=F32)


def prep_kernel(v_ref, wide, wedge, wreg, last, first, local, a_ref, r_ref, pick):
    ch, count, height, width = v_ref.shape
    half = height // 2
    span = ch * half
    depth = 3 * span + edge_rows(ch)

    @pl.when(pl.program_id(0) == 0)
    def _():
        row = lax.broadcasted_iota(jnp.int32, pick.shape, 0)
        col = lax.broadcasted_iota(jnp.int32, pick.shape, 1)
        kind = row // ch
        at = jnp.where(kind == 0, height - 1, jnp.where(kind == 1, 0, jnp.where(kind == 2, half, half - 1)))
        pick[...] = (col == (row % ch) * height + at).astype(F32).astype(BF)

        shape = (ch, half, span)
        diff = lax.broadcasted_iota(jnp.int32, shape, 2) % half - lax.broadcasted_iota(jnp.int32, shape, 1)
        eshape = (ch, half, edge_rows(ch))
        side = (lax.broadcasted_iota(jnp.int32, eshape, 2) // ch) % 2
        keep = lax.broadcasted_iota(jnp.int32, eshape, 1) == side * (half - 1)
        for a in range(3):
            for c in range(3):
                out = jnp.zeros(shape, F32)
                for b in range(3):
                    line = jnp.broadcast_to(wide[9 * a + 3 * b + c][:, None, :], shape)
                    out = jnp.where(diff == b - 1, line, out)
                block = out.reshape(span, span).astype(BF)
                for slot in (a, a + 3):
                    if slot < 5:
                        a_ref[:, slot * depth + c * span : slot * depth + (c + 1) * span] = block
            line = jnp.broadcast_to(wedge[a][:, None, :], eshape)
            block = jnp.where(keep, line, 0.0).reshape(span, edge_rows(ch)).astype(BF)
            for slot in (a, a + 3):
                if slot < 5:
                    a_ref[:, slot * depth + 3 * span : (slot + 1) * depth] = block

        rshape = (height + 8, 2 * span)
        row = lax.broadcasted_iota(jnp.int32, rshape, 0)
        col = lax.broadcasted_iota(jnp.int32, rshape, 1)
        place = jnp.where(
            row < height, row, jnp.where(row == height, -1, jnp.where(row == height + 1, height, -9))
        )
        diff = (col // span) * half + col % half - place
        blocks = []
        for a in range(3):
            for c in range(3):
                out = jnp.zeros(rshape, F32)
                for b in range(3):
                    t = 9 * a + 3 * b + c
                    out = jnp.where(diff == b - 1, jnp.broadcast_to(wreg[t : t + 1, :], rshape), out)
                blocks.append(out)
        r_ref[...] = jnp.concatenate(blocks, axis=0).astype(BF)

    for p in range(count):
        x = v_ref[:, p].reshape(ch * height, width)
        rows = jnp.dot(pick[...], x, preferred_element_type=F32).astype(BF)
        last[p] = rows[:ch]
        first[p] = rows[ch : 2 * ch]
        local[p] = rows[2 * ch :]


def move(x, step):
    width = x.shape[1]
    rolled = pltpu.roll(x, step % width, 1)
    lane = lax.broadcasted_iota(jnp.int32, x.shape, 1)
    return jnp.where(lane == (0 if step == 1 else width - 1), jnp.zeros((), x.dtype), rolled)


def moved(x, step):
    return move(x.astype(F32), step).astype(BF) if step else x


def put_half(x3, slot, x, top, bottom):
    span, ch = x.shape[0], top.shape[0]
    depth = x3.shape[1]
    for k, step in enumerate((1, 0, -1)):
        x3[slot, k * span : (k + 1) * span, :] = moved(x, step)
        base = 3 * span + 2 * k * ch
        x3[slot, base : base + ch, :] = moved(top, step)
        x3[slot, base + ch : base + 2 * ch, :] = moved(bottom, step)
    tail = 3 * span + 6 * ch
    if tail < depth:
        x3[slot, tail:depth, :] = jnp.zeros((depth - tail, x.shape[1]), BF)


def out_plane(phase, a_ref, halves, bias, r_ref, cost, at):
    slots, depth, width = halves[0].shape
    start = phase * depth if isinstance(phase, int) else pl.multiple_of(phase * depth, 128)
    hidden = []
    for x3 in halves:
        a = a_ref[:, pl.ds(start, slots * depth)]
        acc = jnp.dot(a, x3[...].reshape(slots * depth, width), preferred_element_type=F32)
        hidden.append(jnp.maximum(acc + bias[...], 0.0).astype(BF))
    part = jnp.dot(r_ref[...], jnp.concatenate(hidden, axis=0), preferred_element_type=F32)
    rows = cost.shape[1]
    for tap in range(3):
        base = 3 * tap * rows
        total = (
            move(part[base : base + rows], 1)
            + part[base + rows : base + 2 * rows]
            + move(part[base + 2 * rows : base + 3 * rows], -1)
        )
        cost[at + 2 - tap] += total


def flat(x):
    return x.reshape(x.shape[0] * x.shape[1], x.shape[2])


def inner_kernel(lo, hi, above, local, below, a_ref, bias, r_ref, cost, x_lo, x_hi):
    step = pl.program_id(0)
    ch = above.shape[1]

    @pl.when(step == 0)
    def _():
        cost[...] = jnp.zeros_like(cost)

    slot = lax.rem(step, 3)
    put_half(x_lo, slot, flat(lo[:, 0]), above[0], local[0, :ch])
    put_half(x_hi, slot, flat(hi[:, 0]), local[0, ch:], below[0])

    @pl.when(step >= 2)
    def _():
        first = lax.rem(step + 1, 3)
        out_plane(lax.rem(3 - first, 3), a_ref, (x_lo, x_hi), bias, r_ref, cost, step - 1)


def rim_kernel(planes, lo, hi, b_lo, b_hi, a_lo, a_hi, e_ref, a_ref, bias, r_ref, cost_in, cost, x_lo, x_hi):
    step = pl.program_id(0)
    ch = lo.shape[0]

    @pl.when(step == 0)
    def _():
        cost[...] = cost_in[...]

    slot = lax.rem(step, 3)

    def put(low, high):
        put_half(x_lo, slot, flat(low), e_ref[0, :ch], e_ref[0, ch : 2 * ch])
        put_half(x_hi, slot, flat(high), e_ref[0, 2 * ch : 3 * ch], e_ref[0, 3 * ch :])

    @pl.when(step == 0)
    def _():
        put(b_lo[...], b_hi[...])

    @pl.when(step == 5)
    def _():
        put(a_lo[...], a_hi[...])

    @pl.when((step != 0) & (step != 5))
    def _():
        put(lo[:, 0], hi[:, 0])

    @pl.when(slot == 2)
    def _():
        out_plane(0, a_ref, (x_lo, x_hi), bias, r_ref, cost, jnp.where(step == 2, 0, planes - 1))


def combine(first, second):
    peak = jnp.maximum(first[0], second[0])
    left = jnp.exp(first[0] - peak)
    right = jnp.exp(second[0] - peak)
    return jnp.stack((peak, first[1] * left + second[1] * right, first[2] * left + second[2] * right))


def joined(value, axis):
    count = lax.axis_size(axis)
    if count & (count - 1):
        pieces = lax.all_gather(value, axis)
        running = pieces[0]
        for i in range(1, count):
            running = combine(running, pieces[i])
        return running
    step = 1
    while step < count:
        other = lax.ppermute(value, axis, [(i, i ^ step) for i in range(count)])
        value = combine(value, other)
        step *= 2
    return value


def finish_kernel(planes, cost, out, work, slab, prev, following, stats, taken, final, one, each):
    n = lax.axis_size("disp")
    me = lax.axis_index("disp")
    r = lax.axis_index("rows")
    height, width = out.shape
    across = width // 128

    barrier = pltpu.get_barrier_semaphore()
    pl.semaphore_signal(barrier, inc=1, device_id={"rows": 1 - r}, device_id_type=MESH)
    for j in range(1, n):
        pl.semaphore_signal(barrier, inc=1, device_id={"disp": lax.rem(me + j, n)}, device_id_type=MESH)
    pl.semaphore_wait(barrier, n)

    def send(src, dst, sems, index, where):
        return pltpu.make_async_remote_copy(
            src_ref=src,
            dst_ref=dst,
            send_sem=sems.at[0, index],
            recv_sem=sems.at[1, index],
            device_id=where,
            device_id_type=MESH,
        )

    swap = send(cost.at[:, height : height + 8, :], slab, one, 0, {"rows": 1 - r})
    swap.start()
    work[...] = cost[:, :height, :]
    swap.wait()
    row = lax.broadcasted_iota(jnp.int32, (height, width), 0)
    mine = row == (1 - r) * (height - 1)
    for p in (0, planes + 1):
        line = jnp.broadcast_to(slab[p, pl.ds(r, 1), :], (height, width))
        work[p] += jnp.where(mine, line, 0.0)

    up = send(work.at[planes + 1], prev, one, 1, {"disp": jnp.minimum(me + 1, n - 1)})
    down = send(work.at[0], following, one, 2, {"disp": jnp.maximum(me - 1, 0)})

    @pl.when(me < n - 1)
    def _():
        up.start()

    @pl.when(me > 0)
    def _():
        down.start()

    for p in range(1, planes + 1):
        line = jnp.broadcast_to(slab[p, pl.ds(r, 1), :], (height, width))
        work[p] += jnp.where(mine, line, 0.0)

    @pl.when(me < n - 1)
    def _():
        up.wait_send()
        down.wait_recv()

    @pl.when(me > 0)
    def _():
        down.wait_send()
        up.wait_recv()

    @pl.when(me > 0)
    def _():
        work[1] += prev[...]

    @pl.when(me < n - 1)
    def _():
        work[planes] += following[...]

    low = work[1]
    for p in range(2, planes + 1):
        low = jnp.minimum(low, work[p])
    base = (me * planes).astype(F32)
    total = jnp.zeros((height, width), F32)
    moment = jnp.zeros((height, width), F32)
    for p in range(planes):
        expo = jnp.exp(low - work[p + 1])
        total += expo
        moment += (base + float(p)) * expo
    peak = -low

    def place(k):
        at = (k // across) * 8, (k % across) * 128
        return slice(at[0], at[0] + 8), slice(at[1], at[1] + 128)

    for k in range(n):
        rows, cols = place(k)
        stats[k, 0] = peak[rows, cols]
        stats[k, 1] = total[rows, cols]
        stats[k, 2] = moment[rows, cols]

    copies = []
    for j in range(1, n):
        peer = lax.rem(me + j, n)
        copies.append(send(stats.at[peer], taken.at[j], each, j, {"disp": peer}))
        copies[-1].start()
    for copy in copies:
        copy.wait()
    parts = [stats[me]] + [taken[j] for j in range(1, n)]
    top = parts[0][0]
    for part in parts[1:]:
        top = jnp.maximum(top, part[0])
    total = jnp.zeros_like(top)
    moment = jnp.zeros_like(top)
    for part in parts:
        scale = jnp.exp(part[0] - top)
        total += part[1] * scale
        moment += part[2] * scale
    final[me] = moment / total

    copies = []
    for j in range(1, n):
        peer = lax.rem(me + j, n)
        copies.append(send(final.at[me], final.at[me], each, n + j, {"disp": peer}))
        copies[-1].start()
    for copy in copies:
        copy.wait()
    for k in range(n):
        rows, cols = place(k)
        out[rows, cols] = final[k]


def finish(cost, height):
    planes, width = cost.shape[0] - 2, cost.shape[2]
    n = lax.axis_size("disp")
    return pl.pallas_call(
        functools.partial(finish_kernel, planes),
        in_specs=[pl.BlockSpec(memory_space=pltpu.VMEM)],
        out_specs=pl.BlockSpec(memory_space=pltpu.VMEM),
        out_shape=jax.ShapeDtypeStruct((height, width), F32),
        scratch_shapes=[
            pltpu.VMEM((planes + 2, height, width), F32),
            pltpu.VMEM((planes + 2, 8, width), F32),
            pltpu.VMEM((height, width), F32),
            pltpu.VMEM((height, width), F32),
            pltpu.VMEM((n, 3, 8, 128), F32),
            pltpu.VMEM((n, 3, 8, 128), F32),
            pltpu.VMEM((n, 8, 128), F32),
            pltpu.SemaphoreType.DMA((2, 3)),
            pltpu.SemaphoreType.DMA((2, 2 * n)),
        ],
        compiler_params=pltpu.CompilerParams(collective_id=0, has_side_effects=True),
        name="finish",
    )(cost)


def body(volume, conv_weight, conv_bias, reg_weight):
    ch, planes, height, width = volume.shape
    half = height // 2
    span = ch * half
    rows = height + 8
    depth = 3 * span + edge_rows(ch)

    def whole(x):
        return pl.BlockSpec(x.shape, lambda i: (0,) * len(x.shape), pipeline_mode=pl.Buffered(1))

    def shape(*dims, dtype=BF):
        return jax.ShapeDtypeStruct(dims, dtype)

    wide = spread(conv_weight, half)
    taps = jnp.transpose(conv_weight.reshape(3, 3, 3, ch, ch)[:, ::2], (0, 3, 2, 1, 4)).reshape(3, ch, 6 * ch)
    wedge = jnp.pad(taps, ((0, 0), (0, 0), (0, edge_rows(ch) - 6 * ch))).astype(F32)
    wreg = jnp.tile(spread(reg_weight, half), (1, 2))
    bias = jnp.repeat(conv_bias, half)[:, None]

    group = next(n for n in (4, 3, 2, 1) if planes % n == 0)
    last, first, local, a, r = pl.pallas_call(
        prep_kernel,
        grid=(planes // group,),
        in_specs=[
            pl.BlockSpec((ch, group, height, width), lambda i: (0, i, 0, 0)),
            whole(wide),
            whole(wedge),
            whole(wreg),
        ],
        out_specs=[
            pl.BlockSpec((group, ch, width), lambda i: (i, 0, 0)),
            pl.BlockSpec((group, ch, width), lambda i: (i, 0, 0)),
            pl.BlockSpec((group, 2 * ch, width), lambda i: (i, 0, 0)),
            pl.BlockSpec((span, 5 * depth), lambda i: (0, 0)),
            pl.BlockSpec((9 * rows, 2 * span), lambda i: (0, 0)),
        ],
        out_shape=[
            shape(planes, ch, width),
            shape(planes, ch, width),
            shape(planes, 2 * ch, width),
            shape(span, 5 * depth),
            shape(9 * rows, 2 * span),
        ],
        scratch_shapes=[pltpu.VMEM((4 * ch, ch * height), BF)],
        compiler_params=pltpu.CompilerParams(vmem_limit_bytes=48 << 20),
        cost_estimate=pl.CostEstimate(
            flops=8 * ch * ch * height * width * planes, bytes_accessed=2 * volume.size, transcendentals=0
        ),
        name="prep",
    )(volume, wide, wedge, wreg)

    above = shifted(last, "rows", 1)
    below = shifted(first, "rows", -1)

    def edges(p):
        return jnp.concatenate([above[p], local[p], below[p]], axis=0)

    def packed(p):
        return jnp.concatenate([volume[:, p], edges(p).reshape(4 * ch // height, height, width)], axis=0)

    before = shifted(packed(planes - 1), "disp", 1)
    after = shifted(packed(0), "disp", -1)
    edge_before = before[ch:].reshape(4 * ch, width)
    edge_after = after[ch:].reshape(4 * ch, width)

    cost_shape = shape(planes + 2, rows, width, dtype=F32)
    cost_spec = pl.BlockSpec(cost_shape.shape, lambda i: (0, 0, 0))
    scratch = [pltpu.VMEM((3, depth, width), BF)] * 2
    params = pltpu.CompilerParams(vmem_limit_bytes=48 << 20)
    flops = 4 * span * 3 * depth * width

    cost = pl.pallas_call(
        inner_kernel,
        grid=(planes,),
        in_specs=[
            pl.BlockSpec((ch, 1, half, width), lambda i: (0, i, 0, 0)),
            pl.BlockSpec((ch, 1, half, width), lambda i: (0, i, 1, 0)),
            pl.BlockSpec((1, ch, width), lambda i: (i, 0, 0)),
            pl.BlockSpec((1, 2 * ch, width), lambda i: (i, 0, 0)),
            pl.BlockSpec((1, ch, width), lambda i: (i, 0, 0)),
            whole(a),
            whole(bias),
            whole(r),
        ],
        out_specs=cost_spec,
        out_shape=cost_shape,
        scratch_shapes=scratch,
        compiler_params=params,
        cost_estimate=pl.CostEstimate(
            flops=(planes - 2) * flops, bytes_accessed=2 * volume.size, transcendentals=0
        ),
        name="inner",
    )(volume, volume, above, local, below, a, bias, r)

    def rim_plane(i):
        return jnp.where(i < 3, jnp.maximum(i - 1, 0), jnp.minimum(planes + i - 5, planes - 1))

    rim_e = jnp.stack(
        [edge_before, edges(0), edges(1), edges(planes - 2), edges(planes - 1), edge_after]
    )
    cost = pl.pallas_call(
        functools.partial(rim_kernel, planes),
        grid=(6,),
        in_specs=[
            pl.BlockSpec((ch, 1, half, width), lambda i: (0, rim_plane(i), 0, 0)),
            pl.BlockSpec((ch, 1, half, width), lambda i: (0, rim_plane(i), 1, 0)),
            pl.BlockSpec((ch, half, width), lambda i: (0, 0, 0), pipeline_mode=pl.Buffered(1)),
            pl.BlockSpec((ch, half, width), lambda i: (0, 1, 0), pipeline_mode=pl.Buffered(1)),
            pl.BlockSpec((ch, half, width), lambda i: (0, 0, 0), pipeline_mode=pl.Buffered(1)),
            pl.BlockSpec((ch, half, width), lambda i: (0, 1, 0), pipeline_mode=pl.Buffered(1)),
            pl.BlockSpec((1, 4 * ch, width), lambda i: (i, 0, 0)),
            whole(a),
            whole(bias),
            whole(r),
            whole(cost_shape),
        ],
        out_specs=cost_spec,
        out_shape=cost_shape,
        scratch_shapes=scratch,
        compiler_params=params,
        cost_estimate=pl.CostEstimate(flops=2 * flops, bytes_accessed=2 * volume.size // 4, transcendentals=0),
        name="rim",
    )(volume, volume, before, before, after, after, rim_e, a, bias, r, cost)

    n = lax.axis_size("disp")
    if lax.axis_size("rows") == 2 and height % 8 == 0 and height * width == 1024 * n:
        return finish(cost, height)

    from_before = shifted(cost[planes + 1], "disp", 1)
    from_after = shifted(cost[0], "disp", -1)
    cost = cost[1 : planes + 1]
    cost = cost.at[0].add(from_before).at[planes - 1].add(from_after)
    from_below = shifted(cost[:, height], "rows", -1)
    from_above = shifted(cost[:, height + 1], "rows", 1)
    cost = cost[:, :height]
    cost = cost.at[:, height - 1].add(from_below).at[:, 0].add(from_above)

    score = -cost
    peak = jnp.max(score, axis=0)
    expo = jnp.exp(score - peak[None])
    index = (lax.axis_index("disp") * planes + jnp.arange(planes, dtype=jnp.int32)).astype(F32)
    total = jnp.sum(expo, axis=0)
    moment = jnp.sum(index[:, None, None] * expo, axis=0)
    value = joined(jnp.stack((peak, total, moment)), "disp")
    return value[2] / value[1]


def solution(mesh):
    in_specs = (P(None, "disp", ("tiles", "rows"), None), P(), P(), P())
    out_specs = P(("tiles", "rows"), None)
    return jax.shard_map(body, mesh=mesh, in_specs=in_specs, out_specs=out_specs, check_vma=False)
```

```python
import functools

import jax
import jax.numpy as jnp
from jax import lax
from jax.experimental import pallas as pl
from jax.experimental.pallas import tpu as pltpu
from jax.sharding import PartitionSpec as P

BF = jnp.bfloat16
F32 = jnp.float32
MESH = pl.DeviceIdType.MESH


def shifted(x, axis, step):
    count = lax.axis_size(axis)
    pairs = [(i, i + step) for i in range(count) if 0 <= i + step < count]
    return lax.ppermute(x, axis, pairs)


def edge_rows(ch):
    return -(-6 * ch // 256) * 256


def spread(rows, half):
    ch = rows.shape[-1]
    col = jnp.arange(ch * half)
    onehot = (col[None, :] // half == jnp.arange(ch)[:, None]).astype(BF)
    return jnp.einsum("...c,cg->...g", rows, onehot, preferred_element_type=F32)


def prep_kernel(v_ref, wide, wedge, wreg, last, first, local, a_ref, ae_ref, r_ref, pick):
    ch, count, height, width = v_ref.shape
    half = height // 2
    span = ch * half
    edge = edge_rows(ch)

    @pl.when(pl.program_id(0) == 0)
    def _():
        row = lax.broadcasted_iota(jnp.int32, pick.shape, 0)
        col = lax.broadcasted_iota(jnp.int32, pick.shape, 1)
        kind = row // ch
        at = jnp.where(kind == 0, height - 1, jnp.where(kind == 1, 0, jnp.where(kind == 2, half, half - 1)))
        pick[...] = (col == (row % ch) * height + at).astype(F32).astype(BF)

        order = [0, half - 1] + list(range(1, half - 1))
        at = lax.broadcasted_iota(jnp.int32, (ch, span), 1) % half
        side = (lax.broadcasted_iota(jnp.int32, (ch, edge), 1) // ch) % 2
        for a in range(3):
            for c in range(3):
                lines = [wide[9 * a + 3 * b + c] for b in range(3)]
                for k, h in enumerate(order):
                    out = jnp.zeros((ch, span), F32)
                    for b in range(3):
                        out = jnp.where(at == h + b - 1, lines[b], out)
                    out = out.astype(BF)
                    for slot in range(a, 5, 3):
                        base = slot * 3 * span + c * span
                        a_ref[k * ch : (k + 1) * ch, base : base + span] = out
            for k in range(2):
                out = jnp.where(side == k, wedge[a], 0.0).astype(BF)
                for slot in range(a, 5, 3):
                    ae_ref[k * ch : (k + 1) * ch, slot * edge : (slot + 1) * edge] = out

        rshape = (height + 8, 2 * span)
        row = lax.broadcasted_iota(jnp.int32, rshape, 0)
        col = lax.broadcasted_iota(jnp.int32, rshape, 1)
        place = jnp.where(
            row < height, row, jnp.where(row == height, -1, jnp.where(row == height + 1, height, -9))
        )
        turn = (col % span) // ch
        inside = jnp.where(turn == 0, 0, jnp.where(turn == 1, half - 1, turn - 1))
        diff = (col // span) * half + inside - place
        blocks = []
        for a in range(3):
            for c in range(3):
                out = jnp.zeros(rshape, F32)
                for b in range(3):
                    t = 9 * a + 3 * b + c
                    out = jnp.where(diff == b - 1, jnp.broadcast_to(wreg[t : t + 1, :], rshape), out)
                blocks.append(out)
        r_ref[...] = jnp.concatenate(blocks, axis=0).astype(BF)

    for p in range(count):
        x = v_ref[:, p].reshape(ch * height, width)
        rows = jnp.dot(pick[...], x, preferred_element_type=F32).astype(BF)
        last[p] = rows[:ch]
        first[p] = rows[ch : 2 * ch]
        local[p] = rows[2 * ch :]


def move(x, step):
    width = x.shape[1]
    rolled = pltpu.roll(x, step % width, 1)
    lane = lax.broadcasted_iota(jnp.int32, x.shape, 1)
    return jnp.where(lane == (0 if step == 1 else width - 1), jnp.zeros((), x.dtype), rolled)


def moved(x, step):
    return move(x.astype(F32), step).astype(BF) if step else x


def put_half(x3, xe, slot, x, top, bottom):
    span, ch = x.shape[0], top.shape[0]
    edge = xe.shape[1]
    for k, step in enumerate((1, 0, -1)):
        x3[slot, k * span : (k + 1) * span, :] = moved(x, step)
        base = 2 * k * ch
        xe[slot, base : base + ch, :] = moved(top, step)
        xe[slot, base + ch : base + 2 * ch, :] = moved(bottom, step)
    if 6 * ch < edge:
        xe[slot, 6 * ch : edge, :] = jnp.zeros((edge - 6 * ch, x.shape[1]), BF)


def out_plane(phase, a_ref, ae_ref, halves, bias, r_ref, cost, at):
    def product(matrix, x3):
        slots, depth, width = x3.shape
        start = phase * depth if isinstance(phase, int) else pl.multiple_of(phase * depth, 128)
        x = x3[...].reshape(slots * depth, width)
        return jnp.dot(matrix[:, pl.ds(start, slots * depth)], x, preferred_element_type=F32)

    hidden = []
    for x3, xe in halves:
        acc = product(a_ref, x3) + bias[...]
        extra = product(ae_ref, xe)
        count = extra.shape[0]
        hidden.append(jnp.maximum(acc[:count] + extra, 0.0).astype(BF))
        hidden.append(jnp.maximum(acc[count:], 0.0).astype(BF))
    part = jnp.dot(r_ref[...], jnp.concatenate(hidden, axis=0), preferred_element_type=F32)
    rows = cost.shape[1]
    for tap in range(3):
        base = 3 * tap * rows
        total = (
            move(part[base : base + rows], 1)
            + part[base + rows : base + 2 * rows]
            + move(part[base + 2 * rows : base + 3 * rows], -1)
        )
        cost[at + 2 - tap] += total


def flat(x):
    return x.reshape(x.shape[0] * x.shape[1], x.shape[2])


def inner_kernel(lo, hi, above, local, below, a_ref, ae_ref, bias, r_ref, cost, x_lo, x_hi, e_lo, e_hi):
    step = pl.program_id(0)
    ch = above.shape[1]

    @pl.when(step == 0)
    def _():
        cost[...] = jnp.zeros_like(cost)

    slot = lax.rem(step, 3)
    put_half(x_lo, e_lo, slot, flat(lo[:, 0]), above[0], local[0, :ch])
    put_half(x_hi, e_hi, slot, flat(hi[:, 0]), local[0, ch:], below[0])

    @pl.when(step >= 2)
    def _():
        first = lax.rem(step + 1, 3)
        out_plane(lax.rem(3 - first, 3), a_ref, ae_ref, ((x_lo, e_lo), (x_hi, e_hi)), bias, r_ref, cost, step - 1)


def rim_kernel(planes, lo, hi, b_lo, b_hi, a_lo, a_hi, e_ref, a_ref, ae_ref, bias, r_ref, cost_in, cost, x_lo, x_hi, e_lo, e_hi):
    step = pl.program_id(0)
    ch = lo.shape[0]

    @pl.when(step == 0)
    def _():
        cost[...] = cost_in[...]

    slot = lax.rem(step, 3)

    def put(low, high):
        put_half(x_lo, e_lo, slot, flat(low), e_ref[0, :ch], e_ref[0, ch : 2 * ch])
        put_half(x_hi, e_hi, slot, flat(high), e_ref[0, 2 * ch : 3 * ch], e_ref[0, 3 * ch :])

    @pl.when(step == 0)
    def _():
        put(b_lo[...], b_hi[...])

    @pl.when(step == 5)
    def _():
        put(a_lo[...], a_hi[...])

    @pl.when((step != 0) & (step != 5))
    def _():
        put(lo[:, 0], hi[:, 0])

    @pl.when(slot == 2)
    def _():
        out_plane(0, a_ref, ae_ref, ((x_lo, e_lo), (x_hi, e_hi)), bias, r_ref, cost, jnp.where(step == 2, 0, planes - 1))


def combine(first, second):
    peak = jnp.maximum(first[0], second[0])
    left = jnp.exp(first[0] - peak)
    right = jnp.exp(second[0] - peak)
    return jnp.stack((peak, first[1] * left + second[1] * right, first[2] * left + second[2] * right))


def joined(value, axis):
    count = lax.axis_size(axis)
    if count & (count - 1):
        pieces = lax.all_gather(value, axis)
        running = pieces[0]
        for i in range(1, count):
            running = combine(running, pieces[i])
        return running
    step = 1
    while step < count:
        other = lax.ppermute(value, axis, [(i, i ^ step) for i in range(count)])
        value = combine(value, other)
        step *= 2
    return value


def finish_kernel(planes, cost, out, work, slab, prev, following, stats, taken, final, one, each):
    n = lax.axis_size("disp")
    me = lax.axis_index("disp")
    r = lax.axis_index("rows")
    height, width = out.shape
    across = width // 128

    barrier = pltpu.get_barrier_semaphore()
    pl.semaphore_signal(barrier, inc=1, device_id={"rows": 1 - r}, device_id_type=MESH)
    for j in range(1, n):
        pl.semaphore_signal(barrier, inc=1, device_id={"disp": lax.rem(me + j, n)}, device_id_type=MESH)
    pl.semaphore_wait(barrier, n)

    def send(src, dst, sems, index, where):
        return pltpu.make_async_remote_copy(
            src_ref=src,
            dst_ref=dst,
            send_sem=sems.at[0, index],
            recv_sem=sems.at[1, index],
            device_id=where,
            device_id_type=MESH,
        )

    swap = send(cost.at[:, height : height + 8, :], slab, one, 0, {"rows": 1 - r})
    swap.start()
    work[...] = cost[:, :height, :]
    swap.wait()
    row = lax.broadcasted_iota(jnp.int32, (height, width), 0)
    mine = row == (1 - r) * (height - 1)
    for p in (0, planes + 1):
        line = jnp.broadcast_to(slab[p, pl.ds(r, 1), :], (height, width))
        work[p] += jnp.where(mine, line, 0.0)

    up = send(work.at[planes + 1], prev, one, 1, {"disp": jnp.minimum(me + 1, n - 1)})
    down = send(work.at[0], following, one, 2, {"disp": jnp.maximum(me - 1, 0)})

    @pl.when(me < n - 1)
    def _():
        up.start()

    @pl.when(me > 0)
    def _():
        down.start()

    for p in range(1, planes + 1):
        line = jnp.broadcast_to(slab[p, pl.ds(r, 1), :], (height, width))
        work[p] += jnp.where(mine, line, 0.0)

    @pl.when(me < n - 1)
    def _():
        up.wait_send()
        down.wait_recv()

    @pl.when(me > 0)
    def _():
        down.wait_send()
        up.wait_recv()

    @pl.when(me > 0)
    def _():
        work[1] += prev[...]

    @pl.when(me < n - 1)
    def _():
        work[planes] += following[...]

    low = work[1]
    for p in range(2, planes + 1):
        low = jnp.minimum(low, work[p])
    base = (me * planes).astype(F32)
    total = jnp.zeros((height, width), F32)
    moment = jnp.zeros((height, width), F32)
    for p in range(planes):
        expo = jnp.exp(low - work[p + 1])
        total += expo
        moment += (base + float(p)) * expo
    peak = -low

    def place(k):
        at = (k // across) * 8, (k % across) * 128
        return slice(at[0], at[0] + 8), slice(at[1], at[1] + 128)

    for k in range(n):
        rows, cols = place(k)
        stats[k, 0] = peak[rows, cols]
        stats[k, 1] = total[rows, cols]
        stats[k, 2] = moment[rows, cols]

    copies = []
    for j in range(1, n):
        peer = lax.rem(me + j, n)
        copies.append(send(stats.at[peer], taken.at[j], each, j, {"disp": peer}))
        copies[-1].start()
    for copy in copies:
        copy.wait()
    parts = [stats[me]] + [taken[j] for j in range(1, n)]
    top = parts[0][0]
    for part in parts[1:]:
        top = jnp.maximum(top, part[0])
    total = jnp.zeros_like(top)
    moment = jnp.zeros_like(top)
    for part in parts:
        scale = jnp.exp(part[0] - top)
        total += part[1] * scale
        moment += part[2] * scale
    final[me] = moment / total

    copies = []
    for j in range(1, n):
        peer = lax.rem(me + j, n)
        copies.append(send(final.at[me], final.at[me], each, n + j, {"disp": peer}))
        copies[-1].start()
    for copy in copies:
        copy.wait()
    for k in range(n):
        rows, cols = place(k)
        out[rows, cols] = final[k]


def finish(cost, height):
    planes, width = cost.shape[0] - 2, cost.shape[2]
    n = lax.axis_size("disp")
    return pl.pallas_call(
        functools.partial(finish_kernel, planes),
        in_specs=[pl.BlockSpec(memory_space=pltpu.VMEM)],
        out_specs=pl.BlockSpec(memory_space=pltpu.VMEM),
        out_shape=jax.ShapeDtypeStruct((height, width), F32),
        scratch_shapes=[
            pltpu.VMEM((planes + 2, height, width), F32),
            pltpu.VMEM((planes + 2, 8, width), F32),
            pltpu.VMEM((height, width), F32),
            pltpu.VMEM((height, width), F32),
            pltpu.VMEM((n, 3, 8, 128), F32),
            pltpu.VMEM((n, 3, 8, 128), F32),
            pltpu.VMEM((n, 8, 128), F32),
            pltpu.SemaphoreType.DMA((2, 3)),
            pltpu.SemaphoreType.DMA((2, 2 * n)),
        ],
        compiler_params=pltpu.CompilerParams(collective_id=0, has_side_effects=True),
        name="finish",
    )(cost)


def body(volume, conv_weight, conv_bias, reg_weight):
    ch, planes, height, width = volume.shape
    half = height // 2
    span = ch * half
    rows = height + 8
    edge = edge_rows(ch)
    depth = 3 * span + edge

    def whole(x):
        return pl.BlockSpec(x.shape, lambda i: (0,) * len(x.shape), pipeline_mode=pl.Buffered(1))

    def shape(*dims, dtype=BF):
        return jax.ShapeDtypeStruct(dims, dtype)

    wide = spread(conv_weight, half)
    taps = jnp.transpose(conv_weight.reshape(3, 3, 3, ch, ch)[:, ::2], (0, 3, 2, 1, 4)).reshape(3, ch, 6 * ch)
    wedge = jnp.pad(taps, ((0, 0), (0, 0), (0, edge_rows(ch) - 6 * ch))).astype(F32)
    wreg = jnp.tile(reg_weight.astype(F32), (1, height))
    bias = jnp.tile(conv_bias, half)[:, None]

    group = next(n for n in (4, 3, 2, 1) if planes % n == 0)
    last, first, local, a, ae, r = pl.pallas_call(
        prep_kernel,
        grid=(planes // group,),
        in_specs=[
            pl.BlockSpec((ch, group, height, width), lambda i: (0, i, 0, 0)),
            whole(wide),
            whole(wedge),
            whole(wreg),
        ],
        out_specs=[
            pl.BlockSpec((group, ch, width), lambda i: (i, 0, 0)),
            pl.BlockSpec((group, ch, width), lambda i: (i, 0, 0)),
            pl.BlockSpec((group, 2 * ch, width), lambda i: (i, 0, 0)),
            pl.BlockSpec((span, 15 * span), lambda i: (0, 0)),
            pl.BlockSpec((2 * ch, 5 * edge), lambda i: (0, 0)),
            pl.BlockSpec((9 * rows, 2 * span), lambda i: (0, 0)),
        ],
        out_shape=[
            shape(planes, ch, width),
            shape(planes, ch, width),
            shape(planes, 2 * ch, width),
            shape(span, 15 * span),
            shape(2 * ch, 5 * edge),
            shape(9 * rows, 2 * span),
        ],
        scratch_shapes=[pltpu.VMEM((4 * ch, ch * height), BF)],
        compiler_params=pltpu.CompilerParams(vmem_limit_bytes=48 << 20),
        cost_estimate=pl.CostEstimate(
            flops=8 * ch * ch * height * width * planes, bytes_accessed=2 * volume.size, transcendentals=0
        ),
        name="prep",
    )(volume, wide, wedge, wreg)

    above = shifted(last, "rows", 1)
    below = shifted(first, "rows", -1)

    def edges(p):
        return jnp.concatenate([above[p], local[p], below[p]], axis=0)

    def packed(p):
        return jnp.concatenate([volume[:, p], edges(p).reshape(4 * ch // height, height, width)], axis=0)

    before = shifted(packed(planes - 1), "disp", 1)
    after = shifted(packed(0), "disp", -1)
    edge_before = before[ch:].reshape(4 * ch, width)
    edge_after = after[ch:].reshape(4 * ch, width)

    cost_shape = shape(planes + 2, rows, width, dtype=F32)
    cost_spec = pl.BlockSpec(cost_shape.shape, lambda i: (0, 0, 0))
    scratch = [pltpu.VMEM((3, 3 * span, width), BF)] * 2 + [pltpu.VMEM((3, edge, width), BF)] * 2
    params = pltpu.CompilerParams(vmem_limit_bytes=48 << 20)
    flops = 4 * span * 3 * depth * width

    cost = pl.pallas_call(
        inner_kernel,
        grid=(planes,),
        in_specs=[
            pl.BlockSpec((ch, 1, half, width), lambda i: (0, i, 0, 0)),
            pl.BlockSpec((ch, 1, half, width), lambda i: (0, i, 1, 0)),
            pl.BlockSpec((1, ch, width), lambda i: (i, 0, 0)),
            pl.BlockSpec((1, 2 * ch, width), lambda i: (i, 0, 0)),
            pl.BlockSpec((1, ch, width), lambda i: (i, 0, 0)),
            whole(a),
            whole(ae),
            whole(bias),
            whole(r),
        ],
        out_specs=cost_spec,
        out_shape=cost_shape,
        scratch_shapes=scratch,
        compiler_params=params,
        cost_estimate=pl.CostEstimate(
            flops=(planes - 2) * flops, bytes_accessed=2 * volume.size, transcendentals=0
        ),
        name="inner",
    )(volume, volume, above, local, below, a, ae, bias, r)

    def rim_plane(i):
        return jnp.where(i < 3, jnp.maximum(i - 1, 0), jnp.minimum(planes + i - 5, planes - 1))

    rim_e = jnp.stack(
        [edge_before, edges(0), edges(1), edges(planes - 2), edges(planes - 1), edge_after]
    )
    cost = pl.pallas_call(
        functools.partial(rim_kernel, planes),
        grid=(6,),
        in_specs=[
            pl.BlockSpec((ch, 1, half, width), lambda i: (0, rim_plane(i), 0, 0)),
            pl.BlockSpec((ch, 1, half, width), lambda i: (0, rim_plane(i), 1, 0)),
            pl.BlockSpec((ch, half, width), lambda i: (0, 0, 0), pipeline_mode=pl.Buffered(1)),
            pl.BlockSpec((ch, half, width), lambda i: (0, 1, 0), pipeline_mode=pl.Buffered(1)),
            pl.BlockSpec((ch, half, width), lambda i: (0, 0, 0), pipeline_mode=pl.Buffered(1)),
            pl.BlockSpec((ch, half, width), lambda i: (0, 1, 0), pipeline_mode=pl.Buffered(1)),
            pl.BlockSpec((1, 4 * ch, width), lambda i: (i, 0, 0)),
            whole(a),
            whole(ae),
            whole(bias),
            whole(r),
            whole(cost_shape),
        ],
        out_specs=cost_spec,
        out_shape=cost_shape,
        scratch_shapes=scratch,
        compiler_params=params,
        cost_estimate=pl.CostEstimate(flops=2 * flops, bytes_accessed=2 * volume.size // 4, transcendentals=0),
        name="rim",
    )(volume, volume, before, before, after, after, rim_e, a, ae, bias, r, cost)

    n = lax.axis_size("disp")
    if lax.axis_size("rows") == 2 and height % 8 == 0 and height * width == 1024 * n:
        return finish(cost, height)

    from_before = shifted(cost[planes + 1], "disp", 1)
    from_after = shifted(cost[0], "disp", -1)
    cost = cost[1 : planes + 1]
    cost = cost.at[0].add(from_before).at[planes - 1].add(from_after)
    from_below = shifted(cost[:, height], "rows", -1)
    from_above = shifted(cost[:, height + 1], "rows", 1)
    cost = cost[:, :height]
    cost = cost.at[:, height - 1].add(from_below).at[:, 0].add(from_above)

    score = -cost
    peak = jnp.max(score, axis=0)
    expo = jnp.exp(score - peak[None])
    index = (lax.axis_index("disp") * planes + jnp.arange(planes, dtype=jnp.int32)).astype(F32)
    total = jnp.sum(expo, axis=0)
    moment = jnp.sum(index[:, None, None] * expo, axis=0)
    value = joined(jnp.stack((peak, total, moment)), "disp")
    return value[2] / value[1]


def solution(mesh):
    in_specs = (P(None, "disp", ("tiles", "rows"), None), P(), P(), P())
    out_specs = P(("tiles", "rows"), None)
    return jax.shard_map(body, mesh=mesh, in_specs=in_specs, out_specs=out_specs, check_vma=False)
```

```python
import functools

import jax
import jax.numpy as jnp
from jax import lax
from jax.experimental import pallas as pl
from jax.experimental.pallas import tpu as pltpu
from jax.sharding import PartitionSpec as P

BF = jnp.bfloat16
F32 = jnp.float32
MESH = pl.DeviceIdType.MESH


def shifted(x, axis, step):
    count = lax.axis_size(axis)
    pairs = [(i, i + step) for i in range(count) if 0 <= i + step < count]
    return lax.ppermute(x, axis, pairs)


def edge_rows(ch):
    return -(-6 * ch // 256) * 256


def spread(rows, half):
    ch = rows.shape[-1]
    col = jnp.arange(ch * half)
    onehot = (col[None, :] // half == jnp.arange(ch)[:, None]).astype(BF)
    return jnp.einsum("...c,cg->...g", rows, onehot, preferred_element_type=F32)


def prep_kernel(v_ref, wide, wedge, wreg, last, first, local, a_ref, ae_ref, r_ref, pick):
    ch, count, height, width = v_ref.shape
    half = height // 2
    span = ch * half
    edge = edge_rows(ch)

    @pl.when(pl.program_id(0) == 0)
    def _():
        row = lax.broadcasted_iota(jnp.int32, pick.shape, 0)
        col = lax.broadcasted_iota(jnp.int32, pick.shape, 1)
        kind = row // ch
        at = jnp.where(kind == 0, height - 1, jnp.where(kind == 1, 0, jnp.where(kind == 2, half, half - 1)))
        pick[...] = (col == (row % ch) * height + at).astype(F32).astype(BF)

        order = [0, half - 1] + list(range(1, half - 1))
        at = lax.broadcasted_iota(jnp.int32, (ch, span), 1) % half
        side = (lax.broadcasted_iota(jnp.int32, (ch, edge), 1) // ch) % 2
        for a in range(3):
            for c in range(3):
                lines = [wide[9 * a + 3 * b + c] for b in range(3)]
                for k, h in enumerate(order):
                    out = jnp.zeros((ch, span), F32)
                    for b in range(3):
                        out = jnp.where(at == h + b - 1, lines[b], out)
                    out = out.astype(BF)
                    for slot in range(a, 5, 3):
                        base = slot * 3 * span + c * span
                        a_ref[k * ch : (k + 1) * ch, base : base + span] = out
            for k in range(2):
                out = jnp.where(side == k, wedge[a], 0.0).astype(BF)
                for slot in range(a, 5, 3):
                    ae_ref[k * ch : (k + 1) * ch, slot * edge : (slot + 1) * edge] = out

        rshape = (height + 8, 2 * span)
        row = lax.broadcasted_iota(jnp.int32, rshape, 0)
        col = lax.broadcasted_iota(jnp.int32, rshape, 1)
        place = jnp.where(
            row < height, row, jnp.where(row == height, -1, jnp.where(row == height + 1, height, -9))
        )
        turn = (col % span) // ch
        inside = jnp.where(turn == 0, 0, jnp.where(turn == 1, half - 1, turn - 1))
        diff = (col // span) * half + inside - place
        blocks = []
        for a in range(3):
            for c in range(3):
                out = jnp.zeros(rshape, F32)
                for b in range(3):
                    t = 9 * a + 3 * b + c
                    out = jnp.where(diff == b - 1, jnp.broadcast_to(wreg[t : t + 1, :], rshape), out)
                blocks.append(out)
        r_ref[...] = jnp.concatenate(blocks, axis=0).astype(BF)

    for p in range(count):
        x = v_ref[:, p].reshape(ch * height, width)
        rows = jnp.dot(pick[...], x, preferred_element_type=F32).astype(BF)
        last[p] = rows[:ch]
        first[p] = rows[ch : 2 * ch]
        local[p] = rows[2 * ch :]


def move(x, step):
    width = x.shape[1]
    rolled = pltpu.roll(x, step % width, 1)
    lane = lax.broadcasted_iota(jnp.int32, x.shape, 1)
    return jnp.where(lane == (0 if step == 1 else width - 1), jnp.zeros((), x.dtype), rolled)


def moved(x, step):
    return move(x, step) if step else x


def put_half(x3, xe, slot, x, top, bottom):
    span, ch = x.shape[0], top.shape[0]
    edge = xe.shape[1]
    for k, step in enumerate((1, 0, -1)):
        x3[slot, k * span : (k + 1) * span, :] = moved(x, step)
        base = 2 * k * ch
        xe[slot, base : base + ch, :] = moved(top, step)
        xe[slot, base + ch : base + 2 * ch, :] = moved(bottom, step)
    if 6 * ch < edge:
        xe[slot, 6 * ch : edge, :] = jnp.zeros((edge - 6 * ch, x.shape[1]), BF)


def out_plane(phase, a_ref, ae_ref, halves, bias, r_ref, cost, at):
    def product(matrix, x3):
        slots, depth, width = x3.shape
        start = phase * depth if isinstance(phase, int) else pl.multiple_of(phase * depth, 128)
        x = x3[...].reshape(slots * depth, width)
        return jnp.dot(matrix[:, pl.ds(start, slots * depth)], x, preferred_element_type=F32)

    hidden = []
    for x3, xe in halves:
        acc = product(a_ref, x3) + bias[...]
        extra = product(ae_ref, xe)
        count = extra.shape[0]
        hidden.append(jnp.maximum(acc[:count] + extra, 0.0).astype(BF))
        hidden.append(jnp.maximum(acc[count:], 0.0).astype(BF))
    part = jnp.dot(r_ref[...], jnp.concatenate(hidden, axis=0), preferred_element_type=F32)
    rows = cost.shape[1]
    for tap in range(3):
        base = 3 * tap * rows
        total = (
            move(part[base : base + rows], 1)
            + part[base + rows : base + 2 * rows]
            + move(part[base + 2 * rows : base + 3 * rows], -1)
        )
        cost[at + 2 - tap] += total


def flat(x):
    return x.reshape(x.shape[0] * x.shape[1], x.shape[2])


def inner_kernel(lo, hi, above, local, below, a_ref, ae_ref, bias, r_ref, cost, x_lo, x_hi, e_lo, e_hi):
    step = pl.program_id(0)
    ch = above.shape[1]

    @pl.when(step == 0)
    def _():
        cost[...] = jnp.zeros_like(cost)

    slot = lax.rem(step, 3)
    put_half(x_lo, e_lo, slot, flat(lo[:, 0]), above[0], local[0, :ch])
    put_half(x_hi, e_hi, slot, flat(hi[:, 0]), local[0, ch:], below[0])

    @pl.when(step >= 2)
    def _():
        first = lax.rem(step + 1, 3)
        out_plane(lax.rem(3 - first, 3), a_ref, ae_ref, ((x_lo, e_lo), (x_hi, e_hi)), bias, r_ref, cost, step - 1)


def rim_kernel(planes, lo, hi, b_lo, b_hi, a_lo, a_hi, e_ref, a_ref, ae_ref, bias, r_ref, cost_in, cost, x_lo, x_hi, e_lo, e_hi):
    step = pl.program_id(0)
    ch = lo.shape[0]

    @pl.when(step == 0)
    def _():
        cost[...] = cost_in[...]

    slot = lax.rem(step, 3)

    def put(low, high):
        put_half(x_lo, e_lo, slot, flat(low), e_ref[0, :ch], e_ref[0, ch : 2 * ch])
        put_half(x_hi, e_hi, slot, flat(high), e_ref[0, 2 * ch : 3 * ch], e_ref[0, 3 * ch :])

    @pl.when(step == 0)
    def _():
        put(b_lo[...], b_hi[...])

    @pl.when(step == 5)
    def _():
        put(a_lo[...], a_hi[...])

    @pl.when((step != 0) & (step != 5))
    def _():
        put(lo[:, 0], hi[:, 0])

    @pl.when(slot == 2)
    def _():
        out_plane(0, a_ref, ae_ref, ((x_lo, e_lo), (x_hi, e_hi)), bias, r_ref, cost, jnp.where(step == 2, 0, planes - 1))


def combine(first, second):
    peak = jnp.maximum(first[0], second[0])
    left = jnp.exp(first[0] - peak)
    right = jnp.exp(second[0] - peak)
    return jnp.stack((peak, first[1] * left + second[1] * right, first[2] * left + second[2] * right))


def joined(value, axis):
    count = lax.axis_size(axis)
    if count & (count - 1):
        pieces = lax.all_gather(value, axis)
        running = pieces[0]
        for i in range(1, count):
            running = combine(running, pieces[i])
        return running
    step = 1
    while step < count:
        other = lax.ppermute(value, axis, [(i, i ^ step) for i in range(count)])
        value = combine(value, other)
        step *= 2
    return value


def finish_kernel(planes, cost, out, work, slab, prev, following, stats, taken, final, one, each):
    n = lax.axis_size("disp")
    me = lax.axis_index("disp")
    r = lax.axis_index("rows")
    height, width = out.shape
    across = width // 128

    barrier = pltpu.get_barrier_semaphore()
    pl.semaphore_signal(barrier, inc=1, device_id={"rows": 1 - r}, device_id_type=MESH)
    for j in range(1, n):
        pl.semaphore_signal(barrier, inc=1, device_id={"disp": lax.rem(me + j, n)}, device_id_type=MESH)
    pl.semaphore_wait(barrier, n)

    def send(src, dst, sems, index, where):
        return pltpu.make_async_remote_copy(
            src_ref=src,
            dst_ref=dst,
            send_sem=sems.at[0, index],
            recv_sem=sems.at[1, index],
            device_id=where,
            device_id_type=MESH,
        )

    swap = send(cost.at[:, height : height + 8, :], slab, one, 0, {"rows": 1 - r})
    swap.start()
    work[...] = cost[:, :height, :]
    swap.wait()
    row = lax.broadcasted_iota(jnp.int32, (height, width), 0)
    mine = row == (1 - r) * (height - 1)
    for p in (0, planes + 1):
        line = jnp.broadcast_to(slab[p, pl.ds(r, 1), :], (height, width))
        work[p] += jnp.where(mine, line, 0.0)

    up = send(work.at[planes + 1], prev, one, 1, {"disp": jnp.minimum(me + 1, n - 1)})
    down = send(work.at[0], following, one, 2, {"disp": jnp.maximum(me - 1, 0)})

    @pl.when(me < n - 1)
    def _():
        up.start()

    @pl.when(me > 0)
    def _():
        down.start()

    for p in range(1, planes + 1):
        line = jnp.broadcast_to(slab[p, pl.ds(r, 1), :], (height, width))
        work[p] += jnp.where(mine, line, 0.0)

    @pl.when(me < n - 1)
    def _():
        up.wait_send()
        down.wait_recv()

    @pl.when(me > 0)
    def _():
        down.wait_send()
        up.wait_recv()

    @pl.when(me > 0)
    def _():
        work[1] += prev[...]

    @pl.when(me < n - 1)
    def _():
        work[planes] += following[...]

    low = work[1]
    for p in range(2, planes + 1):
        low = jnp.minimum(low, work[p])
    base = (me * planes).astype(F32)
    total = jnp.zeros((height, width), F32)
    moment = jnp.zeros((height, width), F32)
    for p in range(planes):
        expo = jnp.exp(low - work[p + 1])
        total += expo
        moment += (base + float(p)) * expo
    peak = -low

    def place(k):
        at = (k // across) * 8, (k % across) * 128
        return slice(at[0], at[0] + 8), slice(at[1], at[1] + 128)

    for k in range(n):
        rows, cols = place(k)
        stats[k, 0] = peak[rows, cols]
        stats[k, 1] = total[rows, cols]
        stats[k, 2] = moment[rows, cols]

    copies = []
    for j in range(1, n):
        peer = lax.rem(me + j, n)
        copies.append(send(stats.at[peer], taken.at[j], each, j, {"disp": peer}))
        copies[-1].start()
    for copy in copies:
        copy.wait()
    parts = [stats[me]] + [taken[j] for j in range(1, n)]
    top = parts[0][0]
    for part in parts[1:]:
        top = jnp.maximum(top, part[0])
    total = jnp.zeros_like(top)
    moment = jnp.zeros_like(top)
    for part in parts:
        scale = jnp.exp(part[0] - top)
        total += part[1] * scale
        moment += part[2] * scale
    final[me] = moment / total

    copies = []
    for j in range(1, n):
        peer = lax.rem(me + j, n)
        copies.append(send(final.at[me], final.at[me], each, n + j, {"disp": peer}))
        copies[-1].start()
    for copy in copies:
        copy.wait()
    for k in range(n):
        rows, cols = place(k)
        out[rows, cols] = final[k]


def finish(cost, height):
    planes, width = cost.shape[0] - 2, cost.shape[2]
    n = lax.axis_size("disp")
    return pl.pallas_call(
        functools.partial(finish_kernel, planes),
        in_specs=[pl.BlockSpec(memory_space=pltpu.VMEM)],
        out_specs=pl.BlockSpec(memory_space=pltpu.VMEM),
        out_shape=jax.ShapeDtypeStruct((height, width), F32),
        scratch_shapes=[
            pltpu.VMEM((planes + 2, height, width), F32),
            pltpu.VMEM((planes + 2, 8, width), F32),
            pltpu.VMEM((height, width), F32),
            pltpu.VMEM((height, width), F32),
            pltpu.VMEM((n, 3, 8, 128), F32),
            pltpu.VMEM((n, 3, 8, 128), F32),
            pltpu.VMEM((n, 8, 128), F32),
            pltpu.SemaphoreType.DMA((2, 3)),
            pltpu.SemaphoreType.DMA((2, 2 * n)),
        ],
        compiler_params=pltpu.CompilerParams(collective_id=0, has_side_effects=True),
        name="finish",
    )(cost)


def body(volume, conv_weight, conv_bias, reg_weight):
    ch, planes, height, width = volume.shape
    half = height // 2
    span = ch * half
    rows = height + 8
    edge = edge_rows(ch)
    depth = 3 * span + edge

    def whole(x):
        return pl.BlockSpec(x.shape, lambda i: (0,) * len(x.shape), pipeline_mode=pl.Buffered(1))

    def shape(*dims, dtype=BF):
        return jax.ShapeDtypeStruct(dims, dtype)

    wide = spread(conv_weight, half)
    taps = jnp.transpose(conv_weight.reshape(3, 3, 3, ch, ch)[:, ::2], (0, 3, 2, 1, 4)).reshape(3, ch, 6 * ch)
    wedge = jnp.pad(taps, ((0, 0), (0, 0), (0, edge_rows(ch) - 6 * ch))).astype(F32)
    wreg = jnp.tile(reg_weight.astype(F32), (1, height))
    bias = jnp.tile(conv_bias, half)[:, None]

    group = next(n for n in (4, 3, 2, 1) if planes % n == 0)
    last, first, local, a, ae, r = pl.pallas_call(
        prep_kernel,
        grid=(planes // group,),
        in_specs=[
            pl.BlockSpec((ch, group, height, width), lambda i: (0, i, 0, 0)),
            whole(wide),
            whole(wedge),
            whole(wreg),
        ],
        out_specs=[
            pl.BlockSpec((group, ch, width), lambda i: (i, 0, 0)),
            pl.BlockSpec((group, ch, width), lambda i: (i, 0, 0)),
            pl.BlockSpec((group, 2 * ch, width), lambda i: (i, 0, 0)),
            pl.BlockSpec((span, 15 * span), lambda i: (0, 0)),
            pl.BlockSpec((2 * ch, 5 * edge), lambda i: (0, 0)),
            pl.BlockSpec((9 * rows, 2 * span), lambda i: (0, 0)),
        ],
        out_shape=[
            shape(planes, ch, width),
            shape(planes, ch, width),
            shape(planes, 2 * ch, width),
            shape(span, 15 * span),
            shape(2 * ch, 5 * edge),
            shape(9 * rows, 2 * span),
        ],
        scratch_shapes=[pltpu.VMEM((4 * ch, ch * height), BF)],
        compiler_params=pltpu.CompilerParams(vmem_limit_bytes=48 << 20),
        cost_estimate=pl.CostEstimate(
            flops=8 * ch * ch * height * width * planes, bytes_accessed=2 * volume.size, transcendentals=0
        ),
        name="prep",
    )(volume, wide, wedge, wreg)

    above = shifted(last, "rows", 1)
    below = shifted(first, "rows", -1)

    def edges(p):
        return jnp.concatenate([above[p], local[p], below[p]], axis=0)

    def packed(p):
        return jnp.concatenate([volume[:, p], edges(p).reshape(4 * ch // height, height, width)], axis=0)

    before = shifted(packed(planes - 1), "disp", 1)
    after = shifted(packed(0), "disp", -1)
    edge_before = before[ch:].reshape(4 * ch, width)
    edge_after = after[ch:].reshape(4 * ch, width)

    cost_shape = shape(planes + 2, rows, width, dtype=F32)
    cost_spec = pl.BlockSpec(cost_shape.shape, lambda i: (0, 0, 0))
    scratch = [pltpu.VMEM((3, 3 * span, width), BF)] * 2 + [pltpu.VMEM((3, edge, width), BF)] * 2
    params = pltpu.CompilerParams(vmem_limit_bytes=48 << 20)
    flops = 4 * span * 3 * depth * width

    cost = pl.pallas_call(
        inner_kernel,
        grid=(planes,),
        in_specs=[
            pl.BlockSpec((ch, 1, half, width), lambda i: (0, i, 0, 0)),
            pl.BlockSpec((ch, 1, half, width), lambda i: (0, i, 1, 0)),
            pl.BlockSpec((1, ch, width), lambda i: (i, 0, 0)),
            pl.BlockSpec((1, 2 * ch, width), lambda i: (i, 0, 0)),
            pl.BlockSpec((1, ch, width), lambda i: (i, 0, 0)),
            whole(a),
            whole(ae),
            whole(bias),
            whole(r),
        ],
        out_specs=cost_spec,
        out_shape=cost_shape,
        scratch_shapes=scratch,
        compiler_params=params,
        cost_estimate=pl.CostEstimate(
            flops=(planes - 2) * flops, bytes_accessed=2 * volume.size, transcendentals=0
        ),
        name="inner",
    )(volume, volume, above, local, below, a, ae, bias, r)

    def rim_plane(i):
        return jnp.where(i < 3, jnp.maximum(i - 1, 0), jnp.minimum(planes + i - 5, planes - 1))

    rim_e = jnp.stack(
        [edge_before, edges(0), edges(1), edges(planes - 2), edges(planes - 1), edge_after]
    )
    cost = pl.pallas_call(
        functools.partial(rim_kernel, planes),
        grid=(6,),
        in_specs=[
            pl.BlockSpec((ch, 1, half, width), lambda i: (0, rim_plane(i), 0, 0)),
            pl.BlockSpec((ch, 1, half, width), lambda i: (0, rim_plane(i), 1, 0)),
            pl.BlockSpec((ch, half, width), lambda i: (0, 0, 0), pipeline_mode=pl.Buffered(1)),
            pl.BlockSpec((ch, half, width), lambda i: (0, 1, 0), pipeline_mode=pl.Buffered(1)),
            pl.BlockSpec((ch, half, width), lambda i: (0, 0, 0), pipeline_mode=pl.Buffered(1)),
            pl.BlockSpec((ch, half, width), lambda i: (0, 1, 0), pipeline_mode=pl.Buffered(1)),
            pl.BlockSpec((1, 4 * ch, width), lambda i: (i, 0, 0)),
            whole(a),
            whole(ae),
            whole(bias),
            whole(r),
            whole(cost_shape),
        ],
        out_specs=cost_spec,
        out_shape=cost_shape,
        scratch_shapes=scratch,
        compiler_params=params,
        cost_estimate=pl.CostEstimate(flops=2 * flops, bytes_accessed=2 * volume.size // 4, transcendentals=0),
        name="rim",
    )(volume, volume, before, before, after, after, rim_e, a, ae, bias, r, cost)

    n = lax.axis_size("disp")
    if lax.axis_size("rows") == 2 and height % 8 == 0 and height * width == 1024 * n:
        return finish(cost, height)

    from_before = shifted(cost[planes + 1], "disp", 1)
    from_after = shifted(cost[0], "disp", -1)
    cost = cost[1 : planes + 1]
    cost = cost.at[0].add(from_before).at[planes - 1].add(from_after)
    from_below = shifted(cost[:, height], "rows", -1)
    from_above = shifted(cost[:, height + 1], "rows", 1)
    cost = cost[:, :height]
    cost = cost.at[:, height - 1].add(from_below).at[:, 0].add(from_above)

    score = -cost
    peak = jnp.max(score, axis=0)
    expo = jnp.exp(score - peak[None])
    index = (lax.axis_index("disp") * planes + jnp.arange(planes, dtype=jnp.int32)).astype(F32)
    total = jnp.sum(expo, axis=0)
    moment = jnp.sum(index[:, None, None] * expo, axis=0)
    value = joined(jnp.stack((peak, total, moment)), "disp")
    return value[2] / value[1]


def solution(mesh):
    in_specs = (P(None, "disp", ("tiles", "rows"), None), P(), P(), P())
    out_specs = P(("tiles", "rows"), None)
    return jax.shard_map(body, mesh=mesh, in_specs=in_specs, out_specs=out_specs, check_vma=False)
```
